32 devices in a mesh: ex: 8 (over y, x, core), fsdp: 4 (over z).
Axes of the slice: x: 2, y: 2, z: 4, core: 2. Of those that a mesh axis runs over, the one named last changes fastest.
Arguments:
- tokens: bfloat16 [4096, 4096], P(('ex', 'fsdp')), may hold values from -6 to 6
- cotangent: bfloat16 [4096, 4096], P(('ex', 'fsdp')), may hold values from -6 to 6
- gate_weight: bfloat16 [4096, 14336], P('ex', 'fsdp'), may hold values from -0.09375 to 0.09375
- up_weight: bfloat16 [4096, 14336], P('ex', 'fsdp'), may hold values from -0.09375 to 0.09375
- down_weight: bfloat16 [14336, 4096], P('fsdp', 'ex'), may hold values from -0.046875 to 0.046875
- model_proj: bfloat16 [4096, 128], replicated, may hold values from -0.09375 to 0.09375
- hidden_proj: bfloat16 [14336, 384], P('fsdp'), may hold values from -0.046875 to 0.046875
Outputs:
- features: float32 [8, 8192], P('ex', 'fsdp')
- gram: float32 [8192, 8192], P('fsdp', 'ex')
The draws below stay inside these ranges and needn't reach their ends.
All inputs are finite; a program needn't handle non-finite values.
Results may differ from the reference program's by a relative error of at most 0.0041.
Values may be sent and summed in bfloat16 or wider, within the bound.
A program may use at most 192 MiB of HBM per device.

```python
import math
import jax
import jax.numpy as jnp
from jax import lax

D = 4096
FF = 14336
KA = 64
KB = 128
SEQ = 512
EXAMPLES = 8


def block_levels(stream_key, extent, cuts, low, largest):
    loudness, own = 1.0, jax.random.fold_in(stream_key, 6)
    for position, parts in cuts:
        draws = jnp.exp(jax.random.uniform(jax.random.fold_in(own, position), (parts,), jnp.float32, low / len(cuts), largest / len(cuts)))
        loudness = loudness * jnp.repeat(draws, extent[position] // parts).reshape([-1 if axis == position else 1 for axis in range(len(extent))])
    return loudness


def noise(own_key, dims, spread, reach, cuts=(), kind=jnp.bfloat16):
    entries = spread * jax.random.normal(own_key, dims, jnp.float32)
    if cuts:
        entries = entries * block_levels(own_key, dims, cuts, -0.22, 0.18)
    return jnp.clip(entries, -reach, reach).astype(kind)


def setup_inputs(seed: int = 0) -> dict:
    key_list = jax.random.split(jax.random.key(seed), 8)
    return {
        "tokens": noise(key_list[0], (EXAMPLES * SEQ, D), 1.0, 6.0, ((0, 32),)),
        "cotangent": noise(key_list[1], (EXAMPLES * SEQ, D), 1.0, 6.0, ((0, 32),)),
        "gate_weight": noise(key_list[2], (D, FF), D ** -0.5, 0.09375, ((0, 8), (1, 4))),
        "up_weight": noise(key_list[3], (D, FF), D ** -0.5, 0.09375, ((0, 8), (1, 4))),
        "down_weight": noise(key_list[4], (FF, D), FF ** -0.5, 0.046875, ((0, 4), (1, 8))),
        "model_proj": noise(key_list[5], (D, 2 * KA), D ** -0.5, 0.09375),
        "hidden_proj": noise(key_list[6], (FF, 3 * KB), FF ** -0.5, 0.046875, ((0, 4),)),
    }


def mult(left, right):
    return jnp.dot(left.astype(jnp.float32), right.astype(jnp.float32), precision=lax.Precision.HIGHEST)

def one_example(pair, gate_weight, up_weight, down_weight, model_proj, hidden_proj):
    rows_in, rows_cot = pair
    gate = mult(rows_in, gate_weight)
    up = mult(rows_in, up_weight)
    sig = jax.nn.sigmoid(gate)
    active = gate * sig
    hidden = (active * up).astype(jnp.bfloat16)
    grad_hidden = mult(rows_cot, down_weight.T)
    d_gate = (grad_hidden * up * sig * (1.0 + gate * (1.0 - sig))).astype(jnp.bfloat16)
    d_up = (grad_hidden * active).astype(jnp.bfloat16)
    proj_in = mult(rows_in, model_proj[:, :KA])
    proj_cot = mult(rows_cot, model_proj[:, KA:])
    proj_hidden = mult(hidden, hidden_proj[:, :KB])
    proj_grad = mult(d_gate, hidden_proj[:, KB:2 * KB])
    proj_grad = proj_grad + mult(d_up, hidden_proj[:, 2 * KB:])
    feature = jnp.dot(proj_in.T, proj_grad, precision=lax.Precision.HIGHEST)
    feature = feature + jnp.dot(proj_cot.T, proj_hidden, precision=lax.Precision.HIGHEST)
    return (feature / math.sqrt(SEQ)).reshape(KA * KB)

def reference(tokens, cotangent, gate_weight, up_weight, down_weight, model_proj, hidden_proj):
    rows_in = tokens.reshape(EXAMPLES, SEQ, D)
    rows_cot = cotangent.reshape(EXAMPLES, SEQ, D)
    features = lax.map(lambda pair: one_example(pair, gate_weight, up_weight, down_weight, model_proj, hidden_proj), (rows_in, rows_cot))
    gram = jnp.dot(features.T, features, precision=lax.Precision.HIGHEST) / EXAMPLES
    return (features, gram)
```

```python
import math

import jax
import jax.numpy as jnp
from jax import lax
from jax.sharding import PartitionSpec as P

KA = 64
KB = 128
SEQ = 512
F32 = jnp.float32


def swap(value, bit, size):
    return lax.ppermute(value, "ex", [(i, i ^ bit) for i in range(size)])


def spread(own, crossed, top, size):
    held = [(0, own), (top, crossed)]
    bit = top // 2
    while bit >= 1:
        held = held + [(mask | bit, swap(block, bit, size)) for mask, block in held]
        bit //= 2
    return held


def columns(rows, mask, width):
    start = lax.bitwise_xor(lax.axis_index("ex"), mask) * width
    return lax.dynamic_slice_in_dim(rows, start, width, 1)


def pair_product(left, right, count):
    left_three = left.reshape(count, SEQ, left.shape[1])
    right_three = right.reshape(count, SEQ, right.shape[1])
    return jnp.einsum("esi,esj->eij", left_three, right_three, precision=lax.Precision.HIGHEST)


def body(tokens, cotangent, gate_weight, up_weight, down_weight, model_proj, hidden_proj):
    size = lax.axis_size("ex")
    deep = lax.axis_size("fsdp")
    top = size // 2
    place = lax.axis_index("ex")
    side = place // top
    half = gate_weight.shape[1] // 2
    width = gate_weight.shape[0]

    def halves(weight, axis):
        mine = lax.dynamic_slice_in_dim(weight, side * half, half, axis)
        theirs = lax.dynamic_slice_in_dim(weight, (1 - side) * half, half, axis)
        return mine, theirs

    gate_mine, gate_theirs = halves(gate_weight, 1)
    up_mine, up_theirs = halves(up_weight, 1)
    down_mine, down_theirs = halves(down_weight, 0)

    in_own = lax.all_gather(tokens, "fsdp", axis=0, tiled=True)
    cot_pair = jnp.concatenate([cotangent, swap(cotangent, top, size)], axis=1)
    cot_both = lax.all_gather(cot_pair, "fsdp", axis=0, tiled=True)
    rows = in_own.shape[0]
    dim = in_own.shape[1]
    whole_in = jnp.concatenate([in_own, swap(in_own, top, size)], axis=0)
    whole_cot = jnp.concatenate([cot_both[:, :dim], cot_both[:, dim:]], axis=0)

    gates = spread(gate_mine, swap(gate_theirs, top, size), top, size)
    ups = spread(up_mine, swap(up_theirs, top, size), top, size)
    downs = spread(down_mine, swap(down_theirs, top, size), top, size)

    gate = sum(
        jnp.dot(columns(whole_in, m, width), w, preferred_element_type=F32) for m, w in gates
    )
    up = sum(jnp.dot(columns(whole_in, m, width), w, preferred_element_type=F32) for m, w in ups)
    grad_hidden = sum(
        lax.dot_general(
            columns(whole_cot, m, width), w, (((1,), (1,)), ((), ())), preferred_element_type=F32
        )
        for m, w in downs
    )
    sig = jax.nn.sigmoid(gate)
    active = gate * sig
    hidden = (active * up).astype(jnp.bfloat16)
    d_gate = (grad_hidden * up * sig * (1.0 + gate * (1.0 - sig))).astype(jnp.bfloat16)
    d_up = (grad_hidden * active).astype(jnp.bfloat16)
    proj_in = jnp.dot(whole_in, model_proj[:, :KA], preferred_element_type=F32)
    proj_cot = jnp.dot(whole_cot, model_proj[:, KA:], preferred_element_type=F32)
    hp = lax.dynamic_slice_in_dim(hidden_proj, side * half, half, 0)
    proj_hidden = jnp.dot(hidden, hp[:, :KB], preferred_element_type=F32)
    proj_grad = jnp.dot(d_gate, hp[:, KB : 2 * KB], preferred_element_type=F32)
    proj_grad = proj_grad + jnp.dot(d_up, hp[:, 2 * KB :], preferred_element_type=F32)
    count = rows // SEQ
    part = pair_product(proj_in, proj_grad, 2 * count) + pair_product(
        proj_cot, proj_hidden, 2 * count
    )
    part = (part * (1.0 / math.sqrt(SEQ))).reshape(2, count, KA * KB)
    every = jnp.zeros((size * count, KA * KB), F32)
    every = lax.dynamic_update_slice_in_dim(every, part[0], place * count, 0)
    every = lax.dynamic_update_slice_in_dim(every, part[1], lax.bitwise_xor(place, top) * count, 0)
    every = lax.psum(every, ("ex", "fsdp"))
    row_width = KA * KB // deep
    col_width = KA * KB // size
    left = lax.dynamic_slice_in_dim(every, lax.axis_index("fsdp") * row_width, row_width, 1)
    right = lax.dynamic_slice_in_dim(every, place * col_width, col_width, 1)
    features = lax.dynamic_slice_in_dim(left, place * count, count, 0)
    gram = jnp.dot(left.T, right, precision=lax.Precision.HIGHEST) / every.shape[0]
    return (features, gram)


def solution(mesh):
    placed = (
        P(("ex", "fsdp"), None),
        P(("ex", "fsdp"), None),
        P("ex", "fsdp"),
        P("ex", "fsdp"),
        P("fsdp", "ex"),
        P(),
        P("fsdp", None),
    )
    return jax.shard_map(
        body,
        mesh=mesh,
        in_specs=placed,
        out_specs=(P("ex", "fsdp"), P("fsdp", "ex")),
        check_vma=False,
    )
```

```python
import functools
import math

import jax
import jax.numpy as jnp
from jax import lax
from jax.experimental import pallas as pl
from jax.experimental.pallas import tpu as pltpu
from jax.sharding import PartitionSpec as P


KA = 64
KB = 128
SEQ = 512
F32 = jnp.float32
VMEM_BYTES = 60 * 1024 * 1024


def swap(value, bit, size):
    return lax.ppermute(value, "ex", [(i, i ^ bit) for i in range(size)])


def spread(own, crossed, top, size):
    held = [(0, own), (top, crossed)]
    bit = top // 2
    while bit >= 1:
        more = [(mask | bit, swap(block, bit, size)) for mask, block in held]
        held = held + more
        bit //= 2
    return held


def tile_of(half):
    return 256 if half % 256 == 0 else half


def up_kernel(masks, width, place_ref, x_ref, *refs):
    *blocks, out_ref = refs
    total = None
    for mask, block in zip(masks, blocks):
        start = pl.multiple_of((place_ref[0] ^ mask) * width, width)
        piece = jnp.dot(x_ref[:, pl.ds(start, width)], block[...], preferred_element_type=F32)
        total = piece if total is None else total + piece
    out_ref[...] = total


def up_product(rows, held, place):
    half = held[0][1].shape[1]
    width = held[0][1].shape[0]
    tile = tile_of(half)
    masks = tuple(m for m, _ in held)
    return pl.pallas_call(
        functools.partial(up_kernel, masks, width),
        out_shape=jax.ShapeDtypeStruct((rows.shape[0], half), F32),
        grid_spec=pltpu.PrefetchScalarGridSpec(
            num_scalar_prefetch=1,
            grid=(half // tile,),
            in_specs=[pl.BlockSpec(rows.shape, lambda t, p: (0, 0))]
            + [pl.BlockSpec((width, tile), lambda t, p: (0, t)) for _ in held],
            out_specs=pl.BlockSpec((rows.shape[0], tile), lambda t, p: (0, t)),
        ),
        compiler_params=pltpu.CompilerParams(vmem_limit_bytes=VMEM_BYTES),
    )(place, rows, *[b for _, b in held])


def down_kernel(masks, width, place_ref, y_ref, gate_ref, up_ref, proj_ref, *refs):
    *blocks, b_ref, g_ref = refs
    grad = None
    for mask, block in zip(masks, blocks):
        start = pl.multiple_of((place_ref[0] ^ mask) * width, width)
        piece = lax.dot_general(
            y_ref[:, pl.ds(start, width)], block[...], (((1,), (1,)), ((), ())),
            preferred_element_type=F32,
        )
        grad = piece if grad is None else grad + piece
    gate = gate_ref[...]
    up = up_ref[...]
    sig = jax.nn.sigmoid(gate)
    active = gate * sig
    hidden = (active * up).astype(jnp.bfloat16)
    d_gate = (grad * up * sig * (1.0 + gate * (1.0 - sig))).astype(jnp.bfloat16)
    d_up = (grad * active).astype(jnp.bfloat16)
    b = jnp.dot(hidden, proj_ref[:, :KB], preferred_element_type=F32)
    g = jnp.dot(d_gate, proj_ref[:, KB : 2 * KB], preferred_element_type=F32)
    g = g + jnp.dot(d_up, proj_ref[:, 2 * KB :], preferred_element_type=F32)

    @pl.when(pl.program_id(0) == 0)
    def _():
        b_ref[...] = b
        g_ref[...] = g

    @pl.when(pl.program_id(0) > 0)
    def _():
        b_ref[...] += b
        g_ref[...] += g


def down_product(rows, gate, up, proj, held, place):
    half = held[0][1].shape[0]
    width = held[0][1].shape[1]
    tile = tile_of(half)
    masks = tuple(m for m, _ in held)
    count = rows.shape[0]
    return pl.pallas_call(
        functools.partial(down_kernel, masks, width),
        out_shape=[jax.ShapeDtypeStruct((count, KB), F32)] * 2,
        grid_spec=pltpu.PrefetchScalarGridSpec(
            num_scalar_prefetch=1,
            grid=(half // tile,),
            in_specs=[
                pl.BlockSpec(rows.shape, lambda t, p: (0, 0)),
                pl.BlockSpec((count, tile), lambda t, p: (0, t)),
                pl.BlockSpec((count, tile), lambda t, p: (0, t)),
                pl.BlockSpec((tile, proj.shape[1]), lambda t, p: (t, 0)),
            ]
            + [pl.BlockSpec((tile, width), lambda t, p: (t, 0)) for _ in held],
            out_specs=[pl.BlockSpec((count, KB), lambda t, p: (0, 0))] * 2,
        ),
        compiler_params=pltpu.CompilerParams(vmem_limit_bytes=VMEM_BYTES),
    )(place, rows, gate, up, proj, *[b for _, b in held])


def share_kernel(
    size, deep, part_ref, left_ref, right_ref, got, own, send1, recv1, send_a, send_b, left_sem, right_sem
):
    top = size // 2
    group = 2 * deep
    per = group // size
    ex = lax.axis_index("ex")
    z = lax.axis_index("fsdp")
    side = ex // top
    base = ex % top
    me = side * deep + z

    def to(src, dst, ss, rs, dev_ex, dev_z):
        return pltpu.make_async_remote_copy(
            src_ref=src, dst_ref=dst, send_sem=ss, recv_sem=rs,
            device_id={"ex": dev_ex, "fsdp": dev_z},
            device_id_type=pl.DeviceIdType.MESH,
        )

    def first(q, rs):
        return to(
            part_ref.at[q], got.at[me], send1.at[q], rs, (q // deep) * top + base, q % deep
        )

    for k in range(1, group):
        q = (me + k) % group
        first(q, recv1.at[me]).start()
    total = part_ref[me]
    for k in range(1, group):
        q = (me + k) % group
        to(part_ref.at[q], got.at[q], send1.at[q], recv1.at[q], ex, z).wait_recv()
        total = total + got[q]
    own[...] = total

    row_z = me // 2
    col_ex = me // per
    half = me % 2
    slot = me % per

    def row_copy(k):
        return to(own, left_ref.at[base, half], send_a.at[k], left_sem.at[base, half], (ex + k) % size, row_z)

    def col_copy(k):
        return to(own, right_ref.at[base, slot], send_b.at[k], right_sem.at[base, slot], col_ex, (z + k) % deep)

    for k in range(size):
        if k == 0:
            @pl.when(row_z != z)
            def _():
                row_copy(0).start()
        else:
            row_copy(k).start()
    for k in range(deep):
        if k == 0:
            @pl.when(col_ex != ex)
            def _():
                col_copy(0).start()
        else:
            col_copy(k).start()

    @pl.when(row_z == z)
    def _():
        left_ref[base, half] = total

    @pl.when(col_ex == ex)
    def _():
        right_ref[base, slot] = total

    for b in range(top):
        for h in range(2):
            q = 2 * z + h

            @pl.when(jnp.logical_or(b != base, q != me))
            def _():
                to(own, left_ref.at[b, h], send_a.at[0], left_sem.at[b, h], ex, z).wait_recv()

        for r in range(per):
            q = ex * per + r

            @pl.when(jnp.logical_or(b != base, q != me))
            def _():
                to(own, right_ref.at[b, r], send_b.at[0], right_sem.at[b, r], ex, z).wait_recv()

    for k in range(1, group):
        first((me + k) % group, recv1.at[me]).wait_send()
    for k in range(size):
        if k == 0:
            @pl.when(row_z != z)
            def _():
                row_copy(0).wait_send()
        else:
            row_copy(k).wait_send()
    for k in range(deep):
        if k == 0:
            @pl.when(col_ex != ex)
            def _():
                col_copy(0).wait_send()
        else:
            col_copy(k).wait_send()


def share(part, size, deep):
    group, two, chunk = part.shape
    top = size // 2
    per = group // size
    dma = pltpu.SemaphoreType.DMA
    return pl.pallas_call(
        functools.partial(share_kernel, size, deep),
        out_shape=[
            jax.ShapeDtypeStruct((top, 2, two, chunk), F32),
            jax.ShapeDtypeStruct((top, per, two, chunk), F32),
        ],
        in_specs=[pl.BlockSpec(memory_space=pltpu.VMEM)],
        out_specs=[pl.BlockSpec(memory_space=pltpu.VMEM)] * 2,
        scratch_shapes=[
            pltpu.VMEM((group, two, chunk), F32),
            pltpu.VMEM((two, chunk), F32),
            dma((group,)), dma((group,)), dma((size,)), dma((deep,)),
            dma((top, 2)), dma((top, per)),
        ],
        compiler_params=pltpu.CompilerParams(has_side_effects=True),
    )(part)


def pair_product(left, right, count):
    left_three = left.reshape(count, SEQ, left.shape[1])
    right_three = right.reshape(count, SEQ, right.shape[1])
    return jnp.einsum("esi,esj->eij", left_three, right_three, precision=lax.Precision.HIGHEST)


def body(tokens, cotangent, gate_weight, up_weight, down_weight, model_proj, hidden_proj):
    size = lax.axis_size("ex")
    deep = lax.axis_size("fsdp")
    top = size // 2
    place = lax.axis_index("ex")
    side = place // top
    half = gate_weight.shape[1] // 2

    def halves(weight, axis):
        mine = lax.dynamic_slice_in_dim(weight, side * half, half, axis)
        theirs = lax.dynamic_slice_in_dim(weight, (1 - side) * half, half, axis)
        return mine, theirs

    gate_mine, gate_theirs = halves(gate_weight, 1)
    up_mine, up_theirs = halves(up_weight, 1)
    down_mine, down_theirs = halves(down_weight, 0)

    in_own = lax.all_gather(tokens, "fsdp", axis=0, tiled=True)
    cot_pair = jnp.concatenate([cotangent, swap(cotangent, top, size)], axis=1)
    cot_both = lax.all_gather(cot_pair, "fsdp", axis=0, tiled=True)
    dim = in_own.shape[1]
    whole_in = jnp.concatenate([in_own, swap(in_own, top, size)], axis=0)
    whole_cot = jnp.concatenate([cot_both[:, :dim], cot_both[:, dim:]], axis=0)

    gates = spread(gate_mine, swap(gate_theirs, top, size), top, size)
    ups = spread(up_mine, swap(up_theirs, top, size), top, size)
    downs = spread(down_mine, swap(down_theirs, top, size), top, size)

    where = place.astype(jnp.int32).reshape(1)
    gate = up_product(whole_in, gates, where)
    up = up_product(whole_in, ups, where)
    proj_in = jnp.dot(whole_in, model_proj[:, :KA], preferred_element_type=F32)
    proj_cot = jnp.dot(whole_cot, model_proj[:, KA:], preferred_element_type=F32)
    hp = lax.dynamic_slice_in_dim(hidden_proj, side * half, half, 0)
    proj_hidden, proj_grad = down_product(whole_cot, gate, up, hp, downs, where)
    part = pair_product(proj_in, proj_grad, 2) + pair_product(proj_cot, proj_hidden, 2)
    part = (part * (1.0 / math.sqrt(SEQ))).reshape(2, KA * KB)
    part = jnp.where(side == 0, part, part[::-1])
    chunk = KA * KB // (2 * deep)
    part = part.reshape(2, 2 * deep, chunk).transpose(1, 0, 2)
    left, right = share(part, size, deep)
    left = left.transpose(2, 0, 1, 3).reshape(size, 2 * chunk)
    right = right.transpose(2, 0, 1, 3).reshape(size, -1)
    features = lax.dynamic_slice_in_dim(left, place, 1, 0)
    gram = jnp.dot(left.T, right, precision=lax.Precision.HIGHEST) / size
    return (features, gram)


def solution(mesh):
    placed = (
        P(("ex", "fsdp"), None),
        P(("ex", "fsdp"), None),
        P("ex", "fsdp"),
        P("ex", "fsdp"),
        P("fsdp", "ex"),
        P(),
        P("fsdp", None),
    )
    return jax.shard_map(
        body,
        mesh=mesh,
        in_specs=placed,
        out_specs=(P("ex", "fsdp"), P("fsdp", "ex")),
        check_vma=False,
    )
```

```python
import functools
import math

import jax
import jax.numpy as jnp
from jax import lax
from jax.experimental import pallas as pl
from jax.experimental.pallas import tpu as pltpu
from jax.sharding import PartitionSpec as P


KA = 64
KB = 128
SEQ = 512
F32 = jnp.float32
VMEM_BYTES = 60 * 1024 * 1024


def swap(value, bit, size):
    return lax.ppermute(value, "ex", [(i, i ^ bit) for i in range(size)])


def spread(own, crossed, top, size):
    held = [(0, own), (top, crossed)]
    bit = top // 2
    while bit >= 1:
        more = [(mask | bit, swap(block, bit, size)) for mask, block in held]
        held = held + more
        bit //= 2
    return held


def tile_of(half):
    return 256 if half % 256 == 0 else half


def up_kernel(masks, width, place_ref, x_ref, *refs):
    *blocks, out_ref = refs
    total = None
    for mask, block in zip(masks, blocks):
        start = pl.multiple_of((place_ref[0] ^ mask) * width, width)
        piece = jnp.dot(x_ref[:, pl.ds(start, width)], block[...], preferred_element_type=F32)
        total = piece if total is None else total + piece
    out_ref[...] = total


def up_product(rows, held, place):
    half = held[0][1].shape[1]
    width = held[0][1].shape[0]
    tile = tile_of(half)
    masks = tuple(m for m, _ in held)
    return pl.pallas_call(
        functools.partial(up_kernel, masks, width),
        out_shape=jax.ShapeDtypeStruct((rows.shape[0], half), F32),
        grid_spec=pltpu.PrefetchScalarGridSpec(
            num_scalar_prefetch=1,
            grid=(half // tile,),
            in_specs=[pl.BlockSpec(rows.shape, lambda t, p: (0, 0))]
            + [pl.BlockSpec((width, tile), lambda t, p: (0, t)) for _ in held],
            out_specs=pl.BlockSpec((rows.shape[0], tile), lambda t, p: (0, t)),
        ),
        compiler_params=pltpu.CompilerParams(vmem_limit_bytes=VMEM_BYTES),
    )(place, rows, *[b for _, b in held])


def down_dots(masks, width, dim, place_ref, y_ref, blocks):
    sums = [None, None]
    for mask, block in zip(masks, blocks):
        start = pl.multiple_of((place_ref[0] ^ mask) * width, width)
        for k in range(2):
            piece = lax.dot_general(
                y_ref[:, pl.ds(start + k * dim, width)], block[...], (((1,), (1,)), ((), ())),
                preferred_element_type=F32,
            )
            sums[k] = piece if sums[k] is None else sums[k] + piece
    return sums


def part_kernel(masks, width, dim, place_ref, y_ref, *refs):
    *blocks, out_ref = refs
    own, other = down_dots(masks, width, dim, place_ref, y_ref, blocks)
    count = y_ref.shape[0]
    out_ref[:count] = own
    out_ref[count:] = other


def part_product(rows, held, place):
    half, width = held[0][1].shape
    tile = tile_of(half)
    masks = tuple(m for m, _ in held)
    count, dim = 2 * rows.shape[0], rows.shape[1] // 2
    return pl.pallas_call(
        functools.partial(part_kernel, masks, width, dim),
        out_shape=jax.ShapeDtypeStruct((count, half), F32),
        grid_spec=pltpu.PrefetchScalarGridSpec(
            num_scalar_prefetch=1,
            grid=(half // tile,),
            in_specs=[pl.BlockSpec(rows.shape, lambda t, p: (0, 0))]
            + [pl.BlockSpec((tile, width), lambda t, p: (t, 0)) for _ in held],
            out_specs=pl.BlockSpec((count, tile), lambda t, p: (0, t)),
        ),
        compiler_params=pltpu.CompilerParams(vmem_limit_bytes=VMEM_BYTES),
    )(place, rows, *[b for _, b in held])


def last_kernel(masks, width, dim, groups, place_ref, y_ref, part_ref, proj_ref, *refs):
    gates, ups = refs[:groups], refs[groups : 2 * groups]
    *blocks, b_ref, g_ref = refs[2 * groups :]
    own, other = down_dots(masks, width, dim, place_ref, y_ref, blocks)
    count = y_ref.shape[0]
    first = pl.program_id(0) == 0
    at = 0
    for gate_ref, up_ref in zip(gates, ups):
        gate = gate_ref[...]
        up = up_ref[...]
        rows = gate.shape[0]
        fresh = own[at : at + rows] if at < count else other[at - count : at - count + rows]
        grad = part_ref[at : at + rows] + fresh
        sig = jax.nn.sigmoid(gate)
        active = gate * sig
        hidden = (active * up).astype(jnp.bfloat16)
        d_gate = (grad * up * sig * (1.0 + gate * (1.0 - sig))).astype(jnp.bfloat16)
        d_up = (grad * active).astype(jnp.bfloat16)
        b = jnp.dot(hidden, proj_ref[:, :KB], preferred_element_type=F32)
        g = jnp.dot(d_gate, proj_ref[:, KB : 2 * KB], preferred_element_type=F32)
        g = g + jnp.dot(d_up, proj_ref[:, 2 * KB :], preferred_element_type=F32)
        here = pl.ds(at, rows)
        b_ref[here] = jnp.where(first, 0.0, b_ref[here]) + b
        g_ref[here] = jnp.where(first, 0.0, g_ref[here]) + g
        at += rows


def last_product(rows, part, gates, ups, proj, held, place):
    half, width = held[0][1].shape
    tile = tile_of(half)
    masks = tuple(m for m, _ in held)
    count, dim = 2 * rows.shape[0], rows.shape[1] // 2
    return pl.pallas_call(
        functools.partial(last_kernel, masks, width, dim, len(gates)),
        out_shape=[jax.ShapeDtypeStruct((count, KB), F32)] * 2,
        grid_spec=pltpu.PrefetchScalarGridSpec(
            num_scalar_prefetch=1,
            grid=(half // tile,),
            in_specs=[
                pl.BlockSpec(rows.shape, lambda t, p: (0, 0)),
                pl.BlockSpec((count, tile), lambda t, p: (0, t)),
                pl.BlockSpec((tile, proj.shape[1]), lambda t, p: (t, 0)),
            ]
            + [pl.BlockSpec((v.shape[0], tile), lambda t, p: (0, t)) for v in gates + ups]
            + [pl.BlockSpec((tile, width), lambda t, p: (t, 0)) for _ in held],
            out_specs=[pl.BlockSpec((count, KB), lambda t, p: (0, 0))] * 2,
        ),
        compiler_params=pltpu.CompilerParams(vmem_limit_bytes=VMEM_BYTES),
    )(place, rows, part, proj, *gates, *ups, *[b for _, b in held])


def share_kernel(
    size, deep, part_ref, left_ref, right_ref, got, own, send1, recv1, send_a, send_b, left_sem, right_sem
):
    top = size // 2
    group = 2 * deep
    per = group // size
    ex = lax.axis_index("ex")
    z = lax.axis_index("fsdp")
    side = ex // top
    base = ex % top
    me = side * deep + z

    def to(src, dst, ss, rs, dev_ex, dev_z):
        return pltpu.make_async_remote_copy(
            src_ref=src, dst_ref=dst, send_sem=ss, recv_sem=rs,
            device_id={"ex": dev_ex, "fsdp": dev_z},
            device_id_type=pl.DeviceIdType.MESH,
        )

    def first(q, rs):
        return to(
            part_ref.at[q], got.at[me], send1.at[q], rs, (q // deep) * top + base, q % deep
        )

    for k in range(1, group):
        q = (me + k) % group
        first(q, recv1.at[me]).start()
    total = part_ref[me]
    for k in range(1, group):
        q = (me + k) % group
        to(part_ref.at[q], got.at[q], send1.at[q], recv1.at[q], ex, z).wait_recv()
        total = total + got[q]
    own[...] = total

    row_z = me // 2
    col_ex = me // per
    half = me % 2
    slot = me % per

    def row_copy(k):
        return to(own, left_ref.at[base, half], send_a.at[k], left_sem.at[base, half], (ex + k) % size, row_z)

    def col_copy(k):
        return to(own, right_ref.at[base, slot], send_b.at[k], right_sem.at[base, slot], col_ex, (z + k) % deep)

    for k in range(size):
        if k == 0:
            @pl.when(row_z != z)
            def _():
                row_copy(0).start()
        else:
            row_copy(k).start()
    for k in range(deep):
        if k == 0:
            @pl.when(col_ex != ex)
            def _():
                col_copy(0).start()
        else:
            col_copy(k).start()

    @pl.when(row_z == z)
    def _():
        left_ref[base, half] = total

    @pl.when(col_ex == ex)
    def _():
        right_ref[base, slot] = total

    for b in range(top):
        for h in range(2):
            q = 2 * z + h

            @pl.when(jnp.logical_or(b != base, q != me))
            def _():
                to(own, left_ref.at[b, h], send_a.at[0], left_sem.at[b, h], ex, z).wait_recv()

        for r in range(per):
            q = ex * per + r

            @pl.when(jnp.logical_or(b != base, q != me))
            def _():
                to(own, right_ref.at[b, r], send_b.at[0], right_sem.at[b, r], ex, z).wait_recv()

    for k in range(1, group):
        first((me + k) % group, recv1.at[me]).wait_send()
    for k in range(size):
        if k == 0:
            @pl.when(row_z != z)
            def _():
                row_copy(0).wait_send()
        else:
            row_copy(k).wait_send()
    for k in range(deep):
        if k == 0:
            @pl.when(col_ex != ex)
            def _():
                col_copy(0).wait_send()
        else:
            col_copy(k).wait_send()


def share(part, size, deep):
    group, two, chunk = part.shape
    top = size // 2
    per = group // size
    dma = pltpu.SemaphoreType.DMA
    return pl.pallas_call(
        functools.partial(share_kernel, size, deep),
        out_shape=[
            jax.ShapeDtypeStruct((top, 2, two, chunk), F32),
            jax.ShapeDtypeStruct((top, per, two, chunk), F32),
        ],
        in_specs=[pl.BlockSpec(memory_space=pltpu.VMEM)],
        out_specs=[pl.BlockSpec(memory_space=pltpu.VMEM)] * 2,
        scratch_shapes=[
            pltpu.VMEM((group, two, chunk), F32),
            pltpu.VMEM((two, chunk), F32),
            dma((group,)), dma((group,)), dma((size,)), dma((deep,)),
            dma((top, 2)), dma((top, per)),
        ],
        compiler_params=pltpu.CompilerParams(has_side_effects=True),
    )(part)


def pair_product(left, right):
    return jnp.einsum("esi,esj->eij", left, right, precision=lax.Precision.HIGHEST)


def body(tokens, cotangent, gate_weight, up_weight, down_weight, model_proj, hidden_proj):
    size = lax.axis_size("ex")
    deep = lax.axis_size("fsdp")
    top = size // 2
    place = lax.axis_index("ex")
    side = place // top
    half = gate_weight.shape[1] // 2

    def halves(weight, axis):
        mine = lax.dynamic_slice_in_dim(weight, side * half, half, axis)
        theirs = lax.dynamic_slice_in_dim(weight, (1 - side) * half, half, axis)
        return mine, theirs

    gate_mine, gate_theirs = halves(gate_weight, 1)
    up_mine, up_theirs = halves(up_weight, 1)
    down_mine, down_theirs = halves(down_weight, 0)

    in_own = lax.all_gather(tokens, "fsdp", axis=0, tiled=True)
    cot_pair = jnp.concatenate([cotangent, swap(cotangent, top, size)], axis=1)
    cot_both = lax.all_gather(cot_pair, "fsdp", axis=0, tiled=True)
    dim = in_own.shape[1]
    split = in_own.shape[0] // 2
    ins = {
        "own": in_own, "0": swap(in_own[:split], top, size), "1": swap(in_own[split:], top, size)
    }

    gates = spread(gate_mine, swap(gate_theirs, top, size), top, size)
    ups = spread(up_mine, swap(up_theirs, top, size), top, size)
    downs = spread(down_mine, swap(down_theirs, top, size), top, size)

    where = place.astype(jnp.int32).reshape(1)
    late = top | (top // 2)
    part = part_product(cot_both, [h for h in downs if h[0] & late != late], where)
    gate, up, proj_in = [], [], []
    proj_cot = [
        jnp.dot(cot_both[:, k * dim : (k + 1) * dim], model_proj[:, KA:], preferred_element_type=F32)
        for k in range(2)
    ]
    for name, rows in ins.items():
        if name == "1":
            rows, proj_in, proj_cot, up, part = lax.optimization_barrier(
                (rows, proj_in, proj_cot, up, part)
            )
        gate.append(up_product(rows, gates, where))
        up.append(up_product(rows, ups, where))
        proj_in.append(jnp.dot(rows, model_proj[:, :KA], preferred_element_type=F32))
    proj_in = [proj_in[0], jnp.concatenate(proj_in[1:], axis=0)]
    hp = lax.dynamic_slice_in_dim(hidden_proj, side * half, half, 0)
    proj_hidden, proj_grad = last_product(
        cot_both, part, gate, up, hp, [h for h in downs if h[0] & late == late], where
    )
    part = pair_product(jnp.stack(proj_in), proj_grad.reshape(2, SEQ, KB)) + pair_product(
        jnp.stack(proj_cot), proj_hidden.reshape(2, SEQ, KB)
    )
    part = (part * (1.0 / math.sqrt(SEQ))).reshape(2, KA * KB)
    own, other = part[:1], part[1:]
    part = jnp.concatenate([jnp.where(side == 0, own, other), jnp.where(side == 0, other, own)])
    chunk = KA * KB // (2 * deep)
    part = part.reshape(2, 2 * deep, chunk).transpose(1, 0, 2)
    left, right = share(part, size, deep)
    left = left.transpose(2, 0, 1, 3).reshape(size, 2 * chunk)
    right = right.transpose(2, 0, 1, 3).reshape(size, -1)
    features = lax.dynamic_slice_in_dim(left, place, 1, 0)
    gram = jnp.dot(left.T, right, precision=lax.Precision.HIGHEST) / size
    return (features, gram)


def solution(mesh):
    placed = (
        P(("ex", "fsdp"), None),
        P(("ex", "fsdp"), None),
        P("ex", "fsdp"),
        P("ex", "fsdp"),
        P("fsdp", "ex"),
        P(),
        P("fsdp", None),
    )
    return jax.shard_map(
        body,
        mesh=mesh,
        in_specs=placed,
        out_specs=(P("ex", "fsdp"), P("fsdp", "ex")),
        check_vma=False,
    )
```

```python
import functools
import math

import jax
import jax.numpy as jnp
from jax import lax
from jax.experimental import pallas as pl
from jax.experimental.pallas import tpu as pltpu
from jax.sharding import PartitionSpec as P


KA = 64
KB = 128
SEQ = 512
F32 = jnp.float32
VMEM_BYTES = 60 * 1024 * 1024


def swap(value, bit, size):
    return lax.ppermute(value, "ex", [(i, i ^ bit) for i in range(size)])


def spread(own, crossed, top, size):
    held = [(0, own), (top, crossed)]
    bit = top // 2
    while bit >= 1:
        more = [(mask | bit, swap(block, bit, size)) for mask, block in held]
        held = held + more
        bit //= 2
    return held


def tile_of(half):
    return 256 if half % 256 == 0 else half


def up_kernel(masks, width, place_ref, x_ref, *refs):
    *blocks, out_ref = refs
    total = None
    for mask, block in zip(masks, blocks):
        start = pl.multiple_of((place_ref[0] ^ mask) * width, width)
        piece = jnp.dot(x_ref[:, pl.ds(start, width)], block[...], preferred_element_type=F32)
        total = piece if total is None else total + piece
    out_ref[...] = total


def up_product(rows, held, place):
    half = held[0][1].shape[1]
    width = held[0][1].shape[0]
    tile = tile_of(half)
    masks = tuple(m for m, _ in held)
    return pl.pallas_call(
        functools.partial(up_kernel, masks, width),
        out_shape=jax.ShapeDtypeStruct((rows.shape[0], half), F32),
        grid_spec=pltpu.PrefetchScalarGridSpec(
            num_scalar_prefetch=1,
            grid=(half // tile,),
            in_specs=[pl.BlockSpec(rows.shape, lambda t, p: (0, 0))]
            + [pl.BlockSpec((width, tile), lambda t, p: (0, t)) for _ in held],
            out_specs=pl.BlockSpec((rows.shape[0], tile), lambda t, p: (0, t)),
        ),
        compiler_params=pltpu.CompilerParams(vmem_limit_bytes=VMEM_BYTES),
    )(place, rows, *[b for _, b in held])


def down_dots(masks, width, dim, place_ref, y_ref, blocks):
    sums = [None, None]
    for mask, block in zip(masks, blocks):
        start = pl.multiple_of((place_ref[0] ^ mask) * width, width)
        for k in range(2):
            piece = lax.dot_general(
                y_ref[:, pl.ds(start + k * dim, width)], block[...], (((1,), (1,)), ((), ())),
                preferred_element_type=F32,
            )
            sums[k] = piece if sums[k] is None else sums[k] + piece
    return sums


def part_kernel(masks, width, dim, place_ref, y_ref, *refs):
    *blocks, out_ref = refs
    own, other = down_dots(masks, width, dim, place_ref, y_ref, blocks)
    count = y_ref.shape[0]
    out_ref[:count] = own
    out_ref[count:] = other


def part_product(rows, held, place):
    half, width = held[0][1].shape
    tile = tile_of(half)
    masks = tuple(m for m, _ in held)
    count, dim = 2 * rows.shape[0], rows.shape[1] // 2
    return pl.pallas_call(
        functools.partial(part_kernel, masks, width, dim),
        out_shape=jax.ShapeDtypeStruct((count, half), F32),
        grid_spec=pltpu.PrefetchScalarGridSpec(
            num_scalar_prefetch=1,
            grid=(half // tile,),
            in_specs=[pl.BlockSpec(rows.shape, lambda t, p: (0, 0))]
            + [pl.BlockSpec((tile, width), lambda t, p: (t, 0)) for _ in held],
            out_specs=pl.BlockSpec((count, tile), lambda t, p: (0, t)),
        ),
        compiler_params=pltpu.CompilerParams(vmem_limit_bytes=VMEM_BYTES),
    )(place, rows, *[b for _, b in held])


def last_kernel(masks, width, dim, groups, place_ref, y_ref, part_ref, proj_ref, *refs):
    gates, ups = refs[:groups], refs[groups : 2 * groups]
    *blocks, b_ref, g_ref = refs[2 * groups :]
    own, other = down_dots(masks, width, dim, place_ref, y_ref, blocks)
    count = y_ref.shape[0]
    first = pl.program_id(0) == 0
    at = 0
    for gate_ref, up_ref in zip(gates, ups):
        gate = gate_ref[...]
        up = up_ref[...]
        rows = gate.shape[0]
        fresh = own[at : at + rows] if at < count else other[at - count : at - count + rows]
        grad = part_ref[at : at + rows] + fresh
        sig = jax.nn.sigmoid(gate)
        active = gate * sig
        hidden = (active * up).astype(jnp.bfloat16)
        d_gate = (grad * up * sig * (1.0 + gate * (1.0 - sig))).astype(jnp.bfloat16)
        d_up = (grad * active).astype(jnp.bfloat16)
        b = jnp.dot(hidden, proj_ref[:, :KB], preferred_element_type=F32)
        g = jnp.dot(d_gate, proj_ref[:, KB : 2 * KB], preferred_element_type=F32)
        g = g + jnp.dot(d_up, proj_ref[:, 2 * KB :], preferred_element_type=F32)
        here = pl.ds(at, rows)
        b_ref[here] = jnp.where(first, 0.0, b_ref[here]) + b
        g_ref[here] = jnp.where(first, 0.0, g_ref[here]) + g
        at += rows


def last_product(rows, part, gates, ups, proj, held, place):
    half, width = held[0][1].shape
    tile = tile_of(half)
    masks = tuple(m for m, _ in held)
    count, dim = 2 * rows.shape[0], rows.shape[1] // 2
    return pl.pallas_call(
        functools.partial(last_kernel, masks, width, dim, len(gates)),
        out_shape=[jax.ShapeDtypeStruct((count, KB), F32)] * 2,
        grid_spec=pltpu.PrefetchScalarGridSpec(
            num_scalar_prefetch=1,
            grid=(half // tile,),
            in_specs=[
                pl.BlockSpec(rows.shape, lambda t, p: (0, 0)),
                pl.BlockSpec((count, tile), lambda t, p: (0, t)),
                pl.BlockSpec((tile, proj.shape[1]), lambda t, p: (t, 0)),
            ]
            + [pl.BlockSpec((v.shape[0], tile), lambda t, p: (0, t)) for v in gates + ups]
            + [pl.BlockSpec((tile, width), lambda t, p: (t, 0)) for _ in held],
            out_specs=[pl.BlockSpec((count, KB), lambda t, p: (0, 0))] * 2,
        ),
        compiler_params=pltpu.CompilerParams(vmem_limit_bytes=VMEM_BYTES),
    )(place, rows, part, proj, *gates, *ups, *[b for _, b in held])


def share_kernel(
    size, deep, part_ref, left_ref, right_ref, got, own, send1, recv1, send_a, send_b, left_sem, right_sem
):
    top = size // 2
    group = 2 * deep
    per = group // size
    ex = lax.axis_index("ex")
    z = lax.axis_index("fsdp")
    side = ex // top
    base = ex % top
    me = side * deep + z

    def to(src, dst, ss, rs, dev_ex, dev_z):
        return pltpu.make_async_remote_copy(
            src_ref=src, dst_ref=dst, send_sem=ss, recv_sem=rs,
            device_id={"ex": dev_ex, "fsdp": dev_z},
            device_id_type=pl.DeviceIdType.MESH,
        )

    def first(q, rs):
        return to(
            part_ref.at[q], got.at[me], send1.at[q], rs, (q // deep) * top + base, q % deep
        )

    for k in range(1, group):
        q = (me + k) % group
        first(q, recv1.at[me]).start()
    total = part_ref[me]
    for k in range(1, group):
        q = (me + k) % group
        to(part_ref.at[q], got.at[q], send1.at[q], recv1.at[q], ex, z).wait_recv()
        total = total + got[q]
    own[...] = total

    row_z = me // 2
    col_ex = me // per
    half = me % 2
    slot = me % per

    def row_copy(k):
        return to(own, left_ref.at[base, half], send_a.at[k], left_sem.at[base, half], (ex + k) % size, row_z)

    def col_copy(k):
        return to(own, right_ref.at[base, slot], send_b.at[k], right_sem.at[base, slot], col_ex, (z + k) % deep)

    for k in range(size):
        if k == 0:
            @pl.when(row_z != z)
            def _():
                row_copy(0).start()
        else:
            row_copy(k).start()
    for k in range(deep):
        if k == 0:
            @pl.when(col_ex != ex)
            def _():
                col_copy(0).start()
        else:
            col_copy(k).start()

    @pl.when(row_z == z)
    def _():
        left_ref[base, half] = total

    @pl.when(col_ex == ex)
    def _():
        right_ref[base, slot] = total

    for b in range(top):
        for h in range(2):
            q = 2 * z + h

            @pl.when(jnp.logical_or(b != base, q != me))
            def _():
                to(own, left_ref.at[b, h], send_a.at[0], left_sem.at[b, h], ex, z).wait_recv()

        for r in range(per):
            q = ex * per + r

            @pl.when(jnp.logical_or(b != base, q != me))
            def _():
                to(own, right_ref.at[b, r], send_b.at[0], right_sem.at[b, r], ex, z).wait_recv()

    for k in range(1, group):
        first((me + k) % group, recv1.at[me]).wait_send()
    for k in range(size):
        if k == 0:
            @pl.when(row_z != z)
            def _():
                row_copy(0).wait_send()
        else:
            row_copy(k).wait_send()
    for k in range(deep):
        if k == 0:
            @pl.when(col_ex != ex)
            def _():
                col_copy(0).wait_send()
        else:
            col_copy(k).wait_send()


def share(part, size, deep):
    group, two, chunk = part.shape
    top = size // 2
    per = group // size
    dma = pltpu.SemaphoreType.DMA
    return pl.pallas_call(
        functools.partial(share_kernel, size, deep),
        out_shape=[
            jax.ShapeDtypeStruct((top, 2, two, chunk), F32),
            jax.ShapeDtypeStruct((top, per, two, chunk), F32),
        ],
        in_specs=[pl.BlockSpec(memory_space=pltpu.VMEM)],
        out_specs=[pl.BlockSpec(memory_space=pltpu.VMEM)] * 2,
        scratch_shapes=[
            pltpu.VMEM((group, two, chunk), F32),
            pltpu.VMEM((two, chunk), F32),
            dma((group,)), dma((group,)), dma((size,)), dma((deep,)),
            dma((top, 2)), dma((top, per)),
        ],
        compiler_params=pltpu.CompilerParams(has_side_effects=True),
    )(part)


def pair_product(left, right):
    return jnp.einsum("esi,esj->eij", left, right, precision=lax.Precision.HIGHEST)


def pieces(value):
    high = value.astype(jnp.bfloat16)
    rest = value - high.astype(F32)
    mid = rest.astype(jnp.bfloat16)
    low = (rest - mid.astype(F32)).astype(jnp.bfloat16)
    return high, mid, low


def gram_kernel(scale, left_ref, right_ref, out_ref):
    l1, l2, l3 = pieces(left_ref[...])
    r1, r2, r3 = pieces(right_ref[...])
    left = jnp.concatenate([l1, l1, l2, l1, l2, l3], axis=0)
    right = jnp.concatenate([r1, r2, r1, r3, r2, r1], axis=0)
    out = lax.dot_general(left, right, (((0,), (0,)), ((), ())), preferred_element_type=F32)
    out_ref[...] = out * scale


def gram_product(left, right, scale):
    rows, columns = left.shape[1], right.shape[1]
    tile = 256 if rows % 256 == 0 else rows
    return pl.pallas_call(
        functools.partial(gram_kernel, scale),
        out_shape=jax.ShapeDtypeStruct((rows, columns), F32),
        grid=(rows // tile,),
        in_specs=[
            pl.BlockSpec((left.shape[0], tile), lambda t: (0, t)),
            pl.BlockSpec(right.shape, lambda t: (0, 0)),
        ],
        out_specs=pl.BlockSpec((tile, columns), lambda t: (t, 0)),
    )(left, right)


def body(tokens, cotangent, gate_weight, up_weight, down_weight, model_proj, hidden_proj):
    size = lax.axis_size("ex")
    deep = lax.axis_size("fsdp")
    top = size // 2
    place = lax.axis_index("ex")
    side = place // top
    half = gate_weight.shape[1] // 2

    def halves(weight, axis):
        mine = lax.dynamic_slice_in_dim(weight, side * half, half, axis)
        theirs = lax.dynamic_slice_in_dim(weight, (1 - side) * half, half, axis)
        return mine, theirs

    gate_mine, gate_theirs = halves(gate_weight, 1)
    up_mine, up_theirs = halves(up_weight, 1)
    down_mine, down_theirs = halves(down_weight, 0)

    in_own = lax.all_gather(tokens, "fsdp", axis=0, tiled=True)
    cot_pair = jnp.concatenate([cotangent, swap(cotangent, top, size)], axis=1)
    cot_both = lax.all_gather(cot_pair, "fsdp", axis=0, tiled=True)
    dim = in_own.shape[1]
    split = in_own.shape[0] // 2
    ins = {
        "own": in_own, "0": swap(in_own[:split], top, size), "1": swap(in_own[split:], top, size)
    }

    gates = spread(gate_mine, swap(gate_theirs, top, size), top, size)
    ups = spread(up_mine, swap(up_theirs, top, size), top, size)
    downs = spread(down_mine, swap(down_theirs, top, size), top, size)

    where = place.astype(jnp.int32).reshape(1)
    late = top | (top // 2)
    part = part_product(cot_both, [h for h in downs if h[0] & late != late], where)
    gate, up, proj_in = [], [], []
    proj_cot = [
        jnp.dot(cot_both[:, k * dim : (k + 1) * dim], model_proj[:, KA:], preferred_element_type=F32)
        for k in range(2)
    ]
    for name, rows in ins.items():
        if name == "1":
            rows, proj_in, proj_cot, up, part = lax.optimization_barrier(
                (rows, proj_in, proj_cot, up, part)
            )
        gate.append(up_product(rows, gates, where))
        up.append(up_product(rows, ups, where))
        proj_in.append(jnp.dot(rows, model_proj[:, :KA], preferred_element_type=F32))
    proj_in = [proj_in[0], jnp.concatenate(proj_in[1:], axis=0)]
    hp = lax.dynamic_slice_in_dim(hidden_proj, side * half, half, 0)
    proj_hidden, proj_grad = last_product(
        cot_both, part, gate, up, hp, [h for h in downs if h[0] & late == late], where
    )
    part = pair_product(jnp.stack(proj_in), proj_grad.reshape(2, SEQ, KB)) + pair_product(
        jnp.stack(proj_cot), proj_hidden.reshape(2, SEQ, KB)
    )
    part = (part * (1.0 / math.sqrt(SEQ))).reshape(2, KA * KB)
    own, other = part[:1], part[1:]
    part = jnp.concatenate([jnp.where(side == 0, own, other), jnp.where(side == 0, other, own)])
    chunk = KA * KB // (2 * deep)
    part = part.reshape(2, 2 * deep, chunk).transpose(1, 0, 2)
    left, right = share(part, size, deep)
    left = left.transpose(2, 0, 1, 3).reshape(size, 2 * chunk)
    right = right.transpose(2, 0, 1, 3).reshape(size, -1)
    features = lax.dynamic_slice_in_dim(left, place, 1, 0)
    gram = gram_product(left, right, 1.0 / size)
    return (features, gram)


def solution(mesh):
    placed = (
        P(("ex", "fsdp"), None),
        P(("ex", "fsdp"), None),
        P("ex", "fsdp"),
        P("ex", "fsdp"),
        P("fsdp", "ex"),
        P(),
        P("fsdp", None),
    )
    return jax.shard_map(
        body,
        mesh=mesh,
        in_specs=placed,
        out_specs=(P("ex", "fsdp"), P("fsdp", "ex")),
        check_vma=False,
    )
```

```python
import functools
import math

import jax
import jax.numpy as jnp
from jax import lax
from jax.experimental import pallas as pl
from jax.experimental.pallas import tpu as pltpu
from jax.sharding import PartitionSpec as P


KA = 64
KB = 128
SEQ = 512
F32 = jnp.float32
VMEM_BYTES = 60 * 1024 * 1024


def swap(value, bit, size):
    return lax.ppermute(value, "ex", [(i, i ^ bit) for i in range(size)])


def spread(own, crossed, top, size):
    held = [(0, own), (top, crossed)]
    bit = top // 2
    while bit >= 1:
        more = [(mask | bit, swap(block, bit, size)) for mask, block in held]
        held = held + more
        bit //= 2
    return held


def tile_of(half):
    return 256 if half % 256 == 0 else half


def up_kernel(masks, width, place_ref, x_ref, *refs):
    *blocks, out_ref = refs
    total = None
    for mask, block in zip(masks, blocks):
        start = pl.multiple_of((place_ref[0] ^ mask) * width, width)
        piece = jnp.dot(x_ref[:, pl.ds(start, width)], block[...], preferred_element_type=F32)
        total = piece if total is None else total + piece
    out_ref[...] = total


def up_product(rows, held, place):
    half = held[0][1].shape[1]
    width = held[0][1].shape[0]
    tile = tile_of(half)
    masks = tuple(m for m, _ in held)
    return pl.pallas_call(
        functools.partial(up_kernel, masks, width),
        out_shape=jax.ShapeDtypeStruct((rows.shape[0], half), F32),
        grid_spec=pltpu.PrefetchScalarGridSpec(
            num_scalar_prefetch=1,
            grid=(half // tile,),
            in_specs=[pl.BlockSpec(rows.shape, lambda t, p: (0, 0))]
            + [pl.BlockSpec((width, tile), lambda t, p: (0, t)) for _ in held],
            out_specs=pl.BlockSpec((rows.shape[0], tile), lambda t, p: (0, t)),
        ),
        compiler_params=pltpu.CompilerParams(vmem_limit_bytes=VMEM_BYTES),
    )(place, rows, *[b for _, b in held])


def down_dots(masks, width, dim, place_ref, y_ref, blocks):
    sums = [None, None]
    for mask, block in zip(masks, blocks):
        start = pl.multiple_of((place_ref[0] ^ mask) * width, width)
        for k in range(2):
            piece = lax.dot_general(
                y_ref[:, pl.ds(start + k * dim, width)], block[...], (((1,), (1,)), ((), ())),
                preferred_element_type=F32,
            )
            sums[k] = piece if sums[k] is None else sums[k] + piece
    return sums


def part_kernel(masks, width, dim, place_ref, y_ref, *refs):
    *blocks, out_ref = refs
    own, other = down_dots(masks, width, dim, place_ref, y_ref, blocks)
    count = y_ref.shape[0]
    out_ref[:count] = own
    out_ref[count:] = other


def part_product(rows, held, place):
    half, width = held[0][1].shape
    tile = tile_of(half)
    masks = tuple(m for m, _ in held)
    count, dim = 2 * rows.shape[0], rows.shape[1] // 2
    return pl.pallas_call(
        functools.partial(part_kernel, masks, width, dim),
        out_shape=jax.ShapeDtypeStruct((count, half), F32),
        grid_spec=pltpu.PrefetchScalarGridSpec(
            num_scalar_prefetch=1,
            grid=(half // tile,),
            in_specs=[pl.BlockSpec(rows.shape, lambda t, p: (0, 0))]
            + [pl.BlockSpec((tile, width), lambda t, p: (t, 0)) for _ in held],
            out_specs=pl.BlockSpec((count, tile), lambda t, p: (0, t)),
        ),
        compiler_params=pltpu.CompilerParams(vmem_limit_bytes=VMEM_BYTES),
    )(place, rows, *[b for _, b in held])


def last_kernel(masks, width, dim, groups, place_ref, y_ref, part_ref, proj_ref, *refs):
    gates, ups = refs[:groups], refs[groups : 2 * groups]
    *blocks, b_ref, g_ref = refs[2 * groups :]
    own, other = down_dots(masks, width, dim, place_ref, y_ref, blocks)
    fresh = jnp.concatenate([own, other], axis=0)
    first = pl.program_id(0) == 0
    at = 0
    for gate_ref, up_ref in zip(gates, ups):
        gate = gate_ref[...]
        up = up_ref[...]
        rows = gate.shape[0]
        grad = part_ref[at : at + rows] + fresh[at : at + rows]
        sig = jax.nn.sigmoid(gate)
        active = gate * sig
        hidden = (active * up).astype(jnp.bfloat16)
        d_gate = (grad * up * sig * (1.0 + gate * (1.0 - sig))).astype(jnp.bfloat16)
        d_up = (grad * active).astype(jnp.bfloat16)
        b = jnp.dot(hidden, proj_ref[:, :KB], preferred_element_type=F32)
        g = jnp.dot(d_gate, proj_ref[:, KB : 2 * KB], preferred_element_type=F32)
        g = g + jnp.dot(d_up, proj_ref[:, 2 * KB :], preferred_element_type=F32)
        here = pl.ds(at, rows)
        b_ref[here] = jnp.where(first, 0.0, b_ref[here]) + b
        g_ref[here] = jnp.where(first, 0.0, g_ref[here]) + g
        at += rows


def last_product(rows, part, gates, ups, proj, held, place):
    half, width = held[0][1].shape
    tile = tile_of(half)
    masks = tuple(m for m, _ in held)
    count, dim = 2 * rows.shape[0], rows.shape[1] // 2
    return pl.pallas_call(
        functools.partial(last_kernel, masks, width, dim, len(gates)),
        out_shape=[jax.ShapeDtypeStruct((count, KB), F32)] * 2,
        grid_spec=pltpu.PrefetchScalarGridSpec(
            num_scalar_prefetch=1,
            grid=(half // tile,),
            in_specs=[
                pl.BlockSpec(rows.shape, lambda t, p: (0, 0)),
                pl.BlockSpec((count, tile), lambda t, p: (0, t)),
                pl.BlockSpec((tile, proj.shape[1]), lambda t, p: (t, 0)),
            ]
            + [pl.BlockSpec((v.shape[0], tile), lambda t, p: (0, t)) for v in gates + ups]
            + [pl.BlockSpec((tile, width), lambda t, p: (t, 0)) for _ in held],
            out_specs=[pl.BlockSpec((count, KB), lambda t, p: (0, 0))] * 2,
        ),
        compiler_params=pltpu.CompilerParams(vmem_limit_bytes=VMEM_BYTES),
    )(place, rows, part, proj, *gates, *ups, *[b for _, b in held])


def share_kernel(
    size, deep, part_ref, left_ref, right_ref, got, own, send1, recv1, send_a, send_b, left_sem, right_sem
):
    top = size // 2
    group = 2 * deep
    per = group // size
    ex = lax.axis_index("ex")
    z = lax.axis_index("fsdp")
    side = ex // top
    base = ex % top
    me = side * deep + z

    def to(src, dst, ss, rs, dev_ex, dev_z):
        return pltpu.make_async_remote_copy(
            src_ref=src, dst_ref=dst, send_sem=ss, recv_sem=rs,
            device_id={"ex": dev_ex, "fsdp": dev_z},
            device_id_type=pl.DeviceIdType.MESH,
        )

    def first(q, rs):
        return to(
            part_ref.at[q], got.at[me], send1.at[q], rs, (q // deep) * top + base, q % deep
        )

    for k in range(1, group):
        q = (me + k) % group
        first(q, recv1.at[me]).start()
    total = part_ref[me]
    for k in range(1, group):
        q = (me + k) % group
        to(part_ref.at[q], got.at[q], send1.at[q], recv1.at[q], ex, z).wait_recv()
        total = total + got[q]
    own[...] = total

    row_z = me // 2
    col_ex = me // per
    half = me % 2
    slot = me % per

    def row_copy(k):
        return to(own, left_ref.at[base, half], send_a.at[k], left_sem.at[base, half], (ex + k) % size, row_z)

    def col_copy(k):
        return to(own, right_ref.at[base, slot], send_b.at[k], right_sem.at[base, slot], col_ex, (z + k) % deep)

    for k in range(size):
        if k == 0:
            @pl.when(row_z != z)
            def _():
                row_copy(0).start()
        else:
            row_copy(k).start()
    for k in range(deep):
        if k == 0:
            @pl.when(col_ex != ex)
            def _():
                col_copy(0).start()
        else:
            col_copy(k).start()

    @pl.when(row_z == z)
    def _():
        left_ref[base, half] = total

    @pl.when(col_ex == ex)
    def _():
        right_ref[base, slot] = total

    for b in range(top):
        for h in range(2):
            q = 2 * z + h

            @pl.when(jnp.logical_or(b != base, q != me))
            def _():
                to(own, left_ref.at[b, h], send_a.at[0], left_sem.at[b, h], ex, z).wait_recv()

        for r in range(per):
            q = ex * per + r

            @pl.when(jnp.logical_or(b != base, q != me))
            def _():
                to(own, right_ref.at[b, r], send_b.at[0], right_sem.at[b, r], ex, z).wait_recv()

    for k in range(1, group):
        first((me + k) % group, recv1.at[me]).wait_send()
    for k in range(size):
        if k == 0:
            @pl.when(row_z != z)
            def _():
                row_copy(0).wait_send()
        else:
            row_copy(k).wait_send()
    for k in range(deep):
        if k == 0:
            @pl.when(col_ex != ex)
            def _():
                col_copy(0).wait_send()
        else:
            col_copy(k).wait_send()


def share(part, size, deep):
    group, two, chunk = part.shape
    top = size // 2
    per = group // size
    dma = pltpu.SemaphoreType.DMA
    return pl.pallas_call(
        functools.partial(share_kernel, size, deep),
        out_shape=[
            jax.ShapeDtypeStruct((top, 2, two, chunk), F32),
            jax.ShapeDtypeStruct((top, per, two, chunk), F32),
        ],
        in_specs=[pl.BlockSpec(memory_space=pltpu.VMEM)],
        out_specs=[pl.BlockSpec(memory_space=pltpu.VMEM)] * 2,
        scratch_shapes=[
            pltpu.VMEM((group, two, chunk), F32),
            pltpu.VMEM((two, chunk), F32),
            dma((group,)), dma((group,)), dma((size,)), dma((deep,)),
            dma((top, 2)), dma((top, per)),
        ],
        compiler_params=pltpu.CompilerParams(has_side_effects=True),
    )(part)


def pair_product(left, right):
    return jnp.einsum("esi,esj->eij", left, right, precision=lax.Precision.HIGHEST)


def pieces(value):
    high = value.astype(jnp.bfloat16)
    rest = value - high.astype(F32)
    mid = rest.astype(jnp.bfloat16)
    low = (rest - mid.astype(F32)).astype(jnp.bfloat16)
    return high, mid, low


def gram_kernel(scale, left_ref, right_ref, out_ref):
    l1, l2, l3 = pieces(left_ref[...])
    r1, r2, r3 = pieces(right_ref[...])
    left = jnp.concatenate([l1, l1, l2, l1, l2, l3], axis=0)
    right = jnp.concatenate([r1, r2, r1, r3, r2, r1], axis=0)
    out = lax.dot_general(left, right, (((0,), (0,)), ((), ())), preferred_element_type=F32)
    out_ref[...] = out * scale


def gram_product(left, right, scale):
    rows, columns = left.shape[1], right.shape[1]
    tile = 256 if rows % 256 == 0 else rows
    return pl.pallas_call(
        functools.partial(gram_kernel, scale),
        out_shape=jax.ShapeDtypeStruct((rows, columns), F32),
        grid=(rows // tile,),
        in_specs=[
            pl.BlockSpec((left.shape[0], tile), lambda t: (0, t)),
            pl.BlockSpec(right.shape, lambda t: (0, 0)),
        ],
        out_specs=pl.BlockSpec((tile, columns), lambda t: (t, 0)),
    )(left, right)


def body(tokens, cotangent, gate_weight, up_weight, down_weight, model_proj, hidden_proj):
    size = lax.axis_size("ex")
    deep = lax.axis_size("fsdp")
    top = size // 2
    place = lax.axis_index("ex")
    side = place // top
    half = gate_weight.shape[1] // 2

    def halves(weight, axis):
        mine = lax.dynamic_slice_in_dim(weight, side * half, half, axis)
        theirs = lax.dynamic_slice_in_dim(weight, (1 - side) * half, half, axis)
        return mine, theirs

    gate_mine, gate_theirs = halves(gate_weight, 1)
    up_mine, up_theirs = halves(up_weight, 1)
    down_mine, down_theirs = halves(down_weight, 0)

    in_own = lax.all_gather(tokens, "fsdp", axis=0, tiled=True)
    cot_pair = jnp.concatenate([cotangent, swap(cotangent, top, size)], axis=1)
    cot_both = lax.all_gather(cot_pair, "fsdp", axis=0, tiled=True)
    dim = in_own.shape[1]
    split = in_own.shape[0] // 2
    ins = {
        "0": jnp.concatenate([in_own, swap(in_own[:split], top, size)], axis=0),
        "1": swap(in_own[split:], top, size),
    }

    gates = spread(gate_mine, swap(gate_theirs, top, size), top, size)
    ups = spread(up_mine, swap(up_theirs, top, size), top, size)
    first_in = jnp.dot(ins["0"], model_proj[:, :KA], preferred_element_type=F32)
    ins["0"], first_in = lax.optimization_barrier((ins["0"], first_in))
    down_crossed = swap(down_theirs, top, size)
    downs = spread(down_mine, down_crossed, top, size)

    where = place.astype(jnp.int32).reshape(1)
    late = top | (top // 2)
    part = part_product(cot_both, [h for h in downs if h[0] & late != late], where)
    gate, up = [], []
    proj_cot = [
        jnp.dot(cot_both[:, k * dim : (k + 1) * dim], model_proj[:, KA:], preferred_element_type=F32)
        for k in range(2)
    ]
    for name, rows in ins.items():
        if name == "1":
            rows, proj_cot, up, part = lax.optimization_barrier((rows, proj_cot, up, part))
        gate.append(up_product(rows, gates, where))
        up.append(up_product(rows, ups, where))
    last_in = jnp.dot(rows, model_proj[:, :KA], preferred_element_type=F32)
    proj_in = [first_in[: 2 * split], jnp.concatenate([first_in[2 * split :], last_in], axis=0)]
    hp = lax.dynamic_slice_in_dim(hidden_proj, side * half, half, 0)
    proj_hidden, proj_grad = last_product(
        cot_both, part, gate, up, hp, [h for h in downs if h[0] & late == late], where
    )
    part = pair_product(jnp.stack(proj_in), proj_grad.reshape(2, SEQ, KB)) + pair_product(
        jnp.stack(proj_cot), proj_hidden.reshape(2, SEQ, KB)
    )
    part = (part * (1.0 / math.sqrt(SEQ))).reshape(2, KA * KB)
    own, other = part[:1], part[1:]
    part = jnp.concatenate([jnp.where(side == 0, own, other), jnp.where(side == 0, other, own)])
    chunk = KA * KB // (2 * deep)
    part = part.reshape(2, 2 * deep, chunk).transpose(1, 0, 2)
    left, right = share(part, size, deep)
    left = left.transpose(2, 0, 1, 3).reshape(size, 2 * chunk)
    right = right.transpose(2, 0, 1, 3).reshape(size, -1)
    features = lax.dynamic_slice_in_dim(left, place, 1, 0)
    gram = gram_product(left, right, 1.0 / size)
    return (features, gram)


def solution(mesh):
    placed = (
        P(("ex", "fsdp"), None),
        P(("ex", "fsdp"), None),
        P("ex", "fsdp"),
        P("ex", "fsdp"),
        P("fsdp", "ex"),
        P(),
        P("fsdp", None),
    )
    return jax.shard_map(
        body,
        mesh=mesh,
        in_specs=placed,
        out_specs=(P("ex", "fsdp"), P("fsdp", "ex")),
        check_vma=False,
    )
```
